512 devices in a mesh: shard: 16 (over z), group: 32 (over x, y, core).
Axes of the slice: x: 4, y: 4, z: 16, core: 2. Of those that a mesh axis runs over, the one named last changes fastest.
Arguments:
- momentum: bfloat16 [512, 1024, 512], P('group', 'shard'), may hold values from -40 to 40
- gradient: bfloat16 [512, 1024, 512], P('group', 'shard'), may hold values from -300 to 300
- weights: bfloat16 [512, 1024, 512], P('group', 'shard'), may hold values from -0.1875 to 0.1875
- slot_map: int32 [32, 16], P('group'), may hold values from 0 to 7, as said below
- tokens: bfloat16 [16, 32, 256, 1024], P('shard', 'group'), may hold values from -6 to 6
Outputs:
- fresh_state: bfloat16 [512, 1024, 512], P('group', 'shard')
- hidden: bfloat16 [16, 32, 256, 512], P('shard', 'group')
The draws below stay inside these ranges and needn't reach their ends.
Inputs may be any that keep to these rules, and one draw needn't show every extreme that they name: `slot_map`: each row holds every expert-layer of its group at least once and at most four times.
All inputs are finite; a program needn't handle non-finite values.
Results may differ from the reference program's by a relative error of at most 0.014.
Values may be sent and summed in bfloat16 or wider, within the bound.
No kernel may reach another device: no remote copies, remote signals or barrier semaphores. Data moves between devices by JAX's collectives and lax.ppermute only.
A program may use at most 64 MiB of HBM per device.

```python
import math
import jax
import jax.numpy as jnp
from jax import lax

D = 1024
F = 512
ITERS = 5
TOK_DEV = 256
OWNERS = 16
GROUPS = 32
MATRICES = 512


def spread_normal(key, salt, level, ramped):
    keys = jax.random.split(jax.random.fold_in(key, salt), 6)
    base = jax.random.normal(keys[0], (MATRICES, D, F), jnp.float32)
    row_scale = jnp.exp(jax.random.uniform(keys[1], (MATRICES, D, 1), jnp.float32) * math.log(10.0))
    column_scale = jnp.exp(jax.random.uniform(keys[2], (MATRICES, 1, F), jnp.float32) * math.log(10.0))
    factor = jnp.ones((MATRICES, D, 1), jnp.float32)
    if ramped:
        row_place = jnp.arange(D, dtype=jnp.float32)[None, :, None] / D
        matrix_place = jnp.arange(MATRICES, dtype=jnp.float32)[:, None, None] / MATRICES
        group_level = jnp.exp(jax.random.uniform(keys[4], (GROUPS,), jnp.float32, -1.0, 1.0))
        block_level = jnp.exp(jax.random.uniform(keys[5], (OWNERS,), jnp.float32, -1.0, 1.0))
        group_factor = jnp.repeat(group_level, MATRICES // GROUPS).reshape(MATRICES, 1, 1)
        block_factor = jnp.repeat(block_level, D // OWNERS).reshape(1, D, 1)
        factor = jnp.sqrt((1.0 + 2.0 * row_place) * (1.0 + matrix_place)) * group_factor * block_factor
    base = jnp.clip(base, -4.0, 4.0)
    return base * row_scale * column_scale * factor * level


def draw_momentum(key, part):
    return spread_normal(key, 11, 0.0465, False).astype(jnp.bfloat16)


def draw_gradient(key, part):
    return jnp.clip(spread_normal(key, 23, 0.1, True), -300.0, 300.0).astype(jnp.bfloat16)


def draw_slot_map(key, part):
    pairs = OWNERS // 2

    def one_group(group_key):
        first_key, second_key = jax.random.split(group_key)
        spare = jnp.repeat(jnp.arange(pairs, dtype=jnp.int32), 3)
        extra = jax.random.permutation(first_key, spare)[:pairs]
        filled = jnp.concatenate([jnp.arange(pairs, dtype=jnp.int32), extra])
        return jax.random.permutation(second_key, filled)
    return jax.vmap(one_group)(jax.random.split(jax.random.fold_in(key, 37), GROUPS))


def steps_of(stream_key, dims, cuts, least, top_value):
    factor_of, own = 1.0, jax.random.fold_in(stream_key, 6)
    for axis_at, shards_of in cuts:
        heights = jnp.exp(jax.random.uniform(jax.random.fold_in(own, axis_at), (shards_of,), jnp.float32, least / len(cuts), top_value / len(cuts)))
        factor_of = factor_of * jnp.repeat(heights, dims[axis_at] // shards_of).reshape([-1 if axis == axis_at else 1 for axis in range(len(dims))])
    return factor_of


def gaussian(key, shape, spread, reach, shards=(), held_as=jnp.bfloat16):
    values = jax.random.normal(key, shape, jnp.float32) * spread
    if len(shards) > 0:
        values = steps_of(key, shape, shards, -0.22, 0.18) * values
    return jnp.clip(values, min=-reach, max=reach).astype(held_as)


def setup_inputs(seed: int = 0) -> dict:
    key_of = jax.random.split(jax.random.key(seed), 6)
    momentum = draw_momentum(jax.random.fold_in(key_of[5], 71), 0)
    gradient = draw_gradient(jax.random.fold_in(key_of[5], 71), 0)
    weights = gaussian(key_of[2], (MATRICES, D, F), D ** -0.5, 0.1875, ((0, 32), (1, 16)))
    slot_map = draw_slot_map(jax.random.fold_in(key_of[5], 71), 0)
    tokens = gaussian(key_of[4], (OWNERS, GROUPS, TOK_DEV, D), 1.0, 6.0, ((0, 16), (1, 32)))
    return dict(momentum=momentum, gradient=gradient, weights=weights, slot_map=slot_map, tokens=tokens)


coefficients = (3.4445, -4.775, 2.0315)
momentum_decay = 0.95
learning_rate = 0.05
clip_rms = 0.5

def orthogonal(matrix):
    widened = matrix.astype(jnp.float32)
    inverse_norm = 1.0 / (jnp.sqrt(jnp.sum(widened * widened)) + 1e-07)
    iterate = (widened * inverse_norm).astype(jnp.bfloat16)
    for iteration in range(ITERS):
        gram = lax.dot_general(iterate, iterate, (((0,), (0,)), ((), ())), preferred_element_type=jnp.float32).astype(jnp.bfloat16)
        squared = jnp.dot(gram, gram, preferred_element_type=jnp.float32)
        polynomial = (coefficients[1] * gram.astype(jnp.float32) + coefficients[2] * squared).astype(jnp.bfloat16)
        product = jnp.dot(iterate, polynomial, preferred_element_type=jnp.float32)
        iterate = (coefficients[0] * iterate.astype(jnp.float32) + product).astype(jnp.bfloat16)
    return (0.2 * math.sqrt(D) * iterate.astype(jnp.float32)).astype(jnp.bfloat16)

def reference(momentum, gradient, weights, slot_map, tokens):
    widened = gradient.astype(jnp.float32)
    grand_total = jnp.sum(widened * widened)
    clip_factor = jnp.minimum(1.0, clip_rms * math.sqrt(MATRICES * D * F) / jnp.sqrt(grand_total + 1e-06))
    fresh_state = (momentum_decay * momentum.astype(jnp.float32) + clip_factor * widened).astype(jnp.bfloat16)
    update = lax.map(orthogonal, fresh_state)
    new_weights = (weights.astype(jnp.float32) - learning_rate * update.astype(jnp.float32)).astype(jnp.bfloat16)
    starts = (jnp.arange(GROUPS, dtype=jnp.int32)[:, None] * OWNERS + 2 * slot_map.astype(jnp.int32)).T.reshape(-1)
    prompts = tokens.reshape(OWNERS * GROUPS, TOK_DEV, D)

    def prefill(item):
        prompt, first = item
        gate_matrix = lax.dynamic_index_in_dim(new_weights, first, 0, keepdims=False)
        up_matrix = lax.dynamic_index_in_dim(new_weights, first + 1, 0, keepdims=False)
        gate_out = jnp.dot(prompt, gate_matrix, preferred_element_type=jnp.float32)
        up_out = jnp.dot(prompt, up_matrix, preferred_element_type=jnp.float32)
        return (jax.nn.silu(gate_out) * up_out).astype(jnp.bfloat16)
    hidden = lax.map(prefill, (prompts, starts)).reshape(OWNERS, GROUPS, TOK_DEV, F)
    return (fresh_state, hidden)
```

```python
import math

import jax
import jax.numpy as jnp
from jax import lax
from jax.sharding import Mesh
from jax.sharding import PartitionSpec as P

D = 1024
F = 512
ITERS = 5
GROUP = ("group_0", "group_1", "group_2")

coefficients = (3.4445, -4.775, 2.0315)
momentum_decay = 0.95
learning_rate = 0.05
clip_rms = 0.5


def spread(x):
    return lax.all_to_all(x, "shard", split_axis=0, concat_axis=0, tiled=True)


def total_over(value, axes):
    peers = math.prod(lax.axis_size(axis) for axis in axes)
    mine = jnp.broadcast_to(value, (peers, 8, 128))
    theirs = lax.all_to_all(mine, axes, split_axis=0, concat_axis=0, tiled=True)
    return jnp.sum(theirs[:, 0, 0])


def orthogonal(matrix):
    widened = matrix.astype(jnp.float32)
    inverse_norm = 1.0 / (jnp.sqrt(jnp.sum(widened * widened)) + 1e-07)
    iterate = (widened * inverse_norm).astype(jnp.bfloat16)
    for iteration in range(ITERS):
        gram = lax.dot_general(
            iterate, iterate, (((0,), (0,)), ((), ())), preferred_element_type=jnp.float32
        ).astype(jnp.bfloat16)
        squared = jnp.dot(gram, gram, preferred_element_type=jnp.float32)
        polynomial = (
            coefficients[1] * gram.astype(jnp.float32) + coefficients[2] * squared
        ).astype(jnp.bfloat16)
        product = jnp.dot(iterate, polynomial, preferred_element_type=jnp.float32)
        iterate = (coefficients[0] * iterate.astype(jnp.float32) + product).astype(jnp.bfloat16)
    return (0.2 * math.sqrt(D) * iterate.astype(jnp.float32)).astype(jnp.bfloat16)


def stepped(weights, update):
    return (weights.astype(jnp.float32) - learning_rate * update.astype(jnp.float32)).astype(
        jnp.bfloat16
    )


def local(momentum, gradient, weights, slot_map, tokens):
    owners = lax.axis_size("shard")
    every_entry = owners * lax.axis_size(GROUP) * D * F
    rows = weights.shape[1]
    chosen = 2 * slot_map[0]

    def of_slots(x, k):
        return x.at[chosen + k].get(mode="promise_in_bounds")

    old_gate = spread(of_slots(weights, 0)).reshape(D, F)
    widened = gradient.astype(jnp.float32)
    grand_total = total_over(total_over(jnp.sum(widened * widened), ("shard",)), GROUP)
    clip_factor = jnp.minimum(
        1.0, clip_rms * math.sqrt(every_entry) / jnp.sqrt(grand_total + 1e-06)
    )
    fresh_state = (momentum_decay * momentum.astype(jnp.float32) + clip_factor * widened).astype(
        jnp.bfloat16
    )
    state_gate = spread(of_slots(fresh_state, 0)).reshape(D, F)
    state_up = spread(of_slots(fresh_state, 1)).reshape(D, F)
    old_up = spread(of_slots(weights, 1)).reshape(D, F)
    prompt = tokens[0, 0]
    new_gate = stepped(old_gate, orthogonal(state_gate))
    gate_out = jnp.dot(prompt, new_gate, preferred_element_type=jnp.float32)
    new_up = stepped(old_up, orthogonal(state_up))
    up_out = jnp.dot(prompt, new_up, preferred_element_type=jnp.float32)
    hidden = (jax.nn.silu(gate_out) * up_out).astype(jnp.bfloat16)
    return (fresh_state, hidden[None, None])


def solution(mesh):
    split = Mesh(
        mesh.devices.reshape(mesh.shape["shard"], 4, 4, 2),
        ("shard", "group_0", "group_1", "group_2"),
    )
    placed = (
        P(GROUP, "shard", None),
        P(GROUP, "shard", None),
        P(GROUP, "shard", None),
        P(GROUP, None),
        P("shard", GROUP, None, None),
    )
    return jax.shard_map(
        local,
        mesh=split,
        in_specs=placed,
        out_specs=(P(GROUP, "shard", None), P("shard", GROUP, None, None)),
        check_vma=False,
    )
```

```python
import functools
import math

import jax
import jax.numpy as jnp
from jax import lax
from jax.experimental import pallas as pl
from jax.experimental.pallas import tpu as pltpu
from jax.sharding import Mesh
from jax.sharding import PartitionSpec as P


D = 1024
F = 512
ITERS = 5
GROUP = ("group_0", "group_1", "group_2")

coefficients = (3.4445, -4.775, 2.0315)
momentum_decay = 0.95
learning_rate = 0.05
clip_rms = 0.5

FAR = (8, 7, 9, 6, 10)
NEAR = (5, 11, 4, 12, 3, 13, 2, 14, 1, 15)
LATE = (3, 13, 2, 14, 1, 15)


def total_over(value, axes):
    peers = math.prod(lax.axis_size(axis) for axis in axes)
    mine = jnp.broadcast_to(value, (peers, 8, 128))
    theirs = lax.all_to_all(mine, axes, split_axis=0, concat_axis=0, tiled=True)
    return jnp.sum(theirs[:, 0, 0])


def orthogonal_kernel(state_ref, update_ref, iterate_ref):
    rows = iterate_ref.shape[0]
    widened = state_ref[...].reshape(rows, F).astype(jnp.float32)
    inverse_norm = 1.0 / (jnp.sqrt(jnp.sum(widened * widened)) + 1e-07)
    iterate_ref[...] = (widened * inverse_norm).astype(jnp.bfloat16)

    def iteration(_, carry):
        iterate = iterate_ref[...]
        gram = lax.dot_general(
            iterate, iterate, (((0,), (0,)), ((), ())), preferred_element_type=jnp.float32
        ).astype(jnp.bfloat16)
        squared = jnp.dot(gram, gram, preferred_element_type=jnp.float32)
        polynomial = (
            coefficients[1] * gram.astype(jnp.float32) + coefficients[2] * squared
        ).astype(jnp.bfloat16)
        product = jnp.dot(iterate, polynomial, preferred_element_type=jnp.float32)
        iterate_ref[...] = (coefficients[0] * iterate.astype(jnp.float32) + product).astype(
            jnp.bfloat16
        )
        return carry

    lax.fori_loop(0, ITERS, iteration, 0)
    update_ref[...] = (
        (0.2 * math.sqrt(D) * iterate_ref[...].astype(jnp.float32))
        .astype(jnp.bfloat16)
        .reshape(update_ref.shape)
    )


def orthogonal(states):
    shards, matrices, rows, _ = states.shape
    return pl.pallas_call(
        orthogonal_kernel,
        grid=(matrices,),
        in_specs=[pl.BlockSpec((shards, 1, rows, F), lambda k: (0, k, 0, 0))],
        out_specs=pl.BlockSpec((1, shards * rows, F), lambda k: (k, 0, 0)),
        out_shape=jax.ShapeDtypeStruct((matrices, shards * rows, F), jnp.bfloat16),
        scratch_shapes=[pltpu.VMEM((shards * rows, F), jnp.bfloat16)],
        cost_estimate=pl.CostEstimate(flops=13_000_000_000, transcendentals=0, bytes_accessed=4 << 20),
    )(states)


def pick_kernel(slots_ref, position_ref, weights_ref, *out_refs):
    shards = len(out_refs)
    for distance, out_ref in enumerate(out_refs):
        slot = lax.rem(position_ref[0] + distance, shards)
        out_ref[...] = weights_ref[slots_ref[slot]]


def picked_by_distance(slots, position, paired):
    shards = slots.shape[0]
    smem = pl.BlockSpec(memory_space=pltpu.SMEM)
    vmem = pl.BlockSpec(memory_space=pltpu.VMEM)
    return pl.pallas_call(
        pick_kernel,
        in_specs=[smem, smem, vmem],
        out_specs=[vmem] * shards,
        out_shape=[jax.ShapeDtypeStruct(paired.shape[1:], paired.dtype)] * shards,
    )(slots, position, paired)


def add_blocks(position, distances, blocks, prompt_ref, update_ref, outs):
    shards, _, rows = prompt_ref.shape
    for distance, block in zip(distances, blocks, strict=True):
        source = lax.rem(position + (shards - distance), shards)
        at = pl.multiple_of(source * rows, rows)
        part = prompt_ref[source]
        for k in range(2):
            old = block[k].astype(jnp.float32)
            update = update_ref[k, pl.ds(at, rows), :].astype(jnp.float32)
            new = (old - learning_rate * update).astype(jnp.bfloat16)
            product = jnp.dot(part, new, preferred_element_type=jnp.float32)
            outs[k] = product if outs[k] is None else outs[k] + product


def early_kernel(distances, position_ref, prompt_ref, update_ref, *refs):
    *blocks, out_ref = refs
    outs = [None, None]
    add_blocks(position_ref[0], distances, blocks, prompt_ref, update_ref, outs)
    out_ref[0] = outs[0]
    out_ref[1] = outs[1]


def late_kernel(distances, position_ref, prompt_ref, update_ref, sums_ref, *refs):
    *blocks, out_ref = refs
    outs = [sums_ref[0], sums_ref[1]]
    add_blocks(position_ref[0], distances, blocks, prompt_ref, update_ref, outs)
    gate, up = outs
    out_ref[...] = (gate / (1.0 + jnp.exp(-gate)) * up).astype(jnp.bfloat16)


def step_and_prefill(momentum, gradient, weights, slot_map, tokens):
    shards = lax.axis_size("shard")
    every_entry = shards * lax.axis_size(GROUP) * D * F
    rows = weights.shape[1]
    position = lax.axis_index("shard")
    slots = slot_map[0]
    paired = weights.reshape(shards // 2, 2, rows, F)

    at = position.reshape(1).astype(jnp.int32)
    mine = picked_by_distance(slots, at, paired)
    old = {0: mine[0]}
    for distance in (*FAR, *NEAR):
        old[distance] = lax.ppermute(
            mine[distance], "shard", [(k, (k + distance) % shards) for k in range(shards)]
        )

    widened = gradient.astype(jnp.float32)
    grand_total = jnp.sum(widened * widened)
    grand_total = total_over(grand_total, ("shard",))
    grand_total = total_over(grand_total, GROUP)
    clip_factor = jnp.minimum(
        1.0, clip_rms * math.sqrt(every_entry) / jnp.sqrt(grand_total + 1e-06)
    )
    fresh_state = (momentum_decay * momentum.astype(jnp.float32) + clip_factor * widened).astype(
        jnp.bfloat16
    )
    picked = fresh_state.reshape(paired.shape).at[slots].get(mode="promise_in_bounds")
    states = lax.all_to_all(picked, "shard", split_axis=0, concat_axis=0, tiled=True)
    update = orthogonal(states)

    prompt = jnp.moveaxis(tokens[0, 0].reshape(-1, shards, rows), 1, 0)
    early = tuple(d for d in old if d not in LATE)
    smem = pl.BlockSpec(memory_space=pltpu.SMEM)
    vmem = pl.BlockSpec(memory_space=pltpu.VMEM)
    count = prompt.shape[1]
    sums = pl.pallas_call(
        functools.partial(early_kernel, early),
        in_specs=[smem] + [vmem] * (2 + len(early)),
        out_specs=vmem,
        out_shape=jax.ShapeDtypeStruct((2, count, F), jnp.float32),
    )(at, prompt, update, *(old[d] for d in early))
    hidden = pl.pallas_call(
        functools.partial(late_kernel, LATE),
        in_specs=[smem] + [vmem] * (3 + len(LATE)),
        out_specs=vmem,
        out_shape=jax.ShapeDtypeStruct((count, F), jnp.bfloat16),
    )(at, prompt, update, sums, *(old[d] for d in LATE))
    return (fresh_state, hidden[None, None])


def solution(mesh):
    split = Mesh(
        mesh.devices.reshape(mesh.shape["shard"], 4, 4, 2),
        ("shard", "group_0", "group_1", "group_2"),
    )
    placed = (
        P(GROUP, "shard", None),
        P(GROUP, "shard", None),
        P(GROUP, "shard", None),
        P(GROUP, None),
        P("shard", GROUP, None, None),
    )
    return jax.shard_map(
        step_and_prefill,
        mesh=split,
        in_specs=placed,
        out_specs=(P(GROUP, "shard", None), P("shard", GROUP, None, None)),
        check_vma=False,
    )
```

```python
import functools
import math

import jax
import jax.numpy as jnp
from jax import lax
from jax.experimental import pallas as pl
from jax.experimental.pallas import tpu as pltpu
from jax.sharding import Mesh
from jax.sharding import PartitionSpec as P


D = 1024
F = 512
ITERS = 5
GROUP = ("group_0", "group_1", "group_2")

coefficients = (3.4445, -4.775, 2.0315)
momentum_decay = 0.95
learning_rate = 0.05
clip_rms = 0.5

FAR = (8, 7, 9, 6, 10)
NEAR = (5, 11, 4, 12, 3, 13, 2, 14, 1, 15)
LATE = (3, 13, 2, 14, 1, 15)


def squares_kernel(gradient_ref, out_ref, sum_ref):
    step = pl.program_id(0)
    widened = gradient_ref[...].astype(jnp.float32)
    part = jnp.sum((widened * widened).reshape(-1, 8, F), axis=0)

    @pl.when(step == 0)
    def _():
        sum_ref[...] = part

    @pl.when(step > 0)
    def _():
        sum_ref[...] += part

    @pl.when(step == pl.num_programs(0) - 1)
    def _():
        out_ref[...] = jnp.full(out_ref.shape, jnp.sum(sum_ref[...]), jnp.float32)


def sum_of_squares(x, copies):
    flat = x.reshape(-1, F)
    steps = 4
    return pl.pallas_call(
        squares_kernel,
        grid=(steps,),
        in_specs=[pl.BlockSpec((flat.shape[0] // steps, F), lambda i: (i, 0))],
        out_specs=pl.BlockSpec((copies, 8, 128), lambda i: (0, 0, 0)),
        out_shape=jax.ShapeDtypeStruct((copies, 8, 128), jnp.float32),
        scratch_shapes=[pltpu.VMEM((8, F), jnp.float32)],
    )(flat)


def add_kernel(parts_ref, out_ref):
    out_ref[...] = jnp.broadcast_to(jnp.sum(parts_ref[...], axis=0)[None], out_ref.shape)


def added(parts, copies):
    vmem = pl.BlockSpec(memory_space=pltpu.VMEM)
    return pl.pallas_call(
        add_kernel,
        in_specs=[vmem],
        out_specs=vmem,
        out_shape=jax.ShapeDtypeStruct((copies, 8, 128), jnp.float32),
    )(parts)


def everyone(x, axes):
    return lax.all_to_all(x, axes, split_axis=0, concat_axis=0, tiled=True)


def orthogonal_kernel(state_ref, prompt_ref, out_ref, iterate_ref):
    rows = iterate_ref.shape[0]
    widened = state_ref[...].reshape(rows, F).astype(jnp.float32)
    inverse_norm = 1.0 / (jnp.sqrt(jnp.sum(widened * widened)) + 1e-07)
    iterate_ref[...] = (widened * inverse_norm).astype(jnp.bfloat16)

    def iteration(_, carry):
        iterate = iterate_ref[...]
        gram = lax.dot_general(
            iterate, iterate, (((0,), (0,)), ((), ())), preferred_element_type=jnp.float32
        ).astype(jnp.bfloat16)
        squared = jnp.dot(gram, gram, preferred_element_type=jnp.float32)
        polynomial = (
            coefficients[1] * gram.astype(jnp.float32) + coefficients[2] * squared
        ).astype(jnp.bfloat16)
        product = jnp.dot(iterate, polynomial, preferred_element_type=jnp.float32)
        iterate_ref[...] = (coefficients[0] * iterate.astype(jnp.float32) + product).astype(
            jnp.bfloat16
        )
        return carry

    lax.fori_loop(0, ITERS, iteration, 0)
    update = (0.2 * math.sqrt(D) * iterate_ref[...].astype(jnp.float32)).astype(jnp.bfloat16)
    product = jnp.dot(prompt_ref[...], update, preferred_element_type=jnp.float32)
    out_ref[0] = -learning_rate * product


def orthogonal(states, prompt):
    shards, matrices, rows, _ = states.shape
    count = prompt.shape[0]
    return pl.pallas_call(
        orthogonal_kernel,
        grid=(matrices,),
        in_specs=[
            pl.BlockSpec((shards, 1, rows, F), lambda k: (0, k, 0, 0)),
            pl.BlockSpec(prompt.shape, lambda k: (0, 0)),
        ],
        out_specs=pl.BlockSpec((1, count, F), lambda k: (k, 0, 0)),
        out_shape=jax.ShapeDtypeStruct((matrices, count, F), jnp.float32),
        scratch_shapes=[pltpu.VMEM((shards * rows, F), jnp.bfloat16)],
        cost_estimate=pl.CostEstimate(flops=14_000_000_000, transcendentals=0, bytes_accessed=4 << 20),
    )(states, prompt)


def pick_kernel(distances, shards, slots_ref, position_ref, weights_ref, *refs):
    *out_refs, semaphores = refs
    copies = []
    for k, distance in enumerate(distances):
        slot = lax.rem(position_ref[0] + distance, shards)
        copies.append(
            pltpu.make_async_copy(weights_ref.at[slots_ref[slot]], out_refs[k], semaphores.at[k])
        )
    for copy in copies:
        copy.start()
    for copy in copies:
        copy.wait()


def picked_by_distance(slots, position, paired, distances):
    smem = pl.BlockSpec(memory_space=pltpu.SMEM)
    vmem = pl.BlockSpec(memory_space=pltpu.VMEM)
    blocks = pl.pallas_call(
        functools.partial(pick_kernel, distances, slots.shape[0]),
        in_specs=[smem, smem, pl.BlockSpec(memory_space=pl.ANY)],
        out_specs=[vmem] * len(distances),
        out_shape=[jax.ShapeDtypeStruct(paired.shape[1:], paired.dtype)] * len(distances),
        scratch_shapes=[pltpu.SemaphoreType.DMA((len(distances),))],
    )(slots, position, paired)
    return dict(zip(distances, blocks, strict=True))


def add_blocks(position, distances, blocks, prompt_ref, sums_ref):
    shards = prompt_ref.shape[0]
    outs = [sums_ref[0], sums_ref[1]]
    for distance, block in zip(distances, blocks, strict=True):
        part = prompt_ref[lax.rem(position + (shards - distance), shards)]
        for k in range(2):
            outs[k] += jnp.dot(part, block[k], preferred_element_type=jnp.float32)
    return outs


def early_kernel(distances, position_ref, prompt_ref, sums_ref, *refs):
    *blocks, out_ref = refs
    gate, up = add_blocks(position_ref[0], distances, blocks, prompt_ref, sums_ref)
    out_ref[0] = gate
    out_ref[1] = up


def late_kernel(distances, position_ref, prompt_ref, sums_ref, *refs):
    *blocks, out_ref = refs
    gate, up = add_blocks(position_ref[0], distances, blocks, prompt_ref, sums_ref)
    out_ref[...] = (gate / (1.0 + jnp.exp(-gate)) * up).astype(jnp.bfloat16)


def step_and_prefill(momentum, gradient, weights, slot_map, tokens):
    shards = lax.axis_size("shard")
    every_entry = shards * lax.axis_size(GROUP) * D * F
    rows = weights.shape[1]
    position = lax.axis_index("shard")
    slots = slot_map[0]
    paired = weights.reshape(shards // 2, 2, rows, F)

    at = position.reshape(1).astype(jnp.int32)
    mine = picked_by_distance(slots, at, paired, FAR)
    mine |= picked_by_distance(slots, at, paired, (0, *NEAR))
    old = {0: mine[0]}
    for distance in (*FAR, *NEAR):
        old[distance] = lax.ppermute(
            mine[distance], "shard", [(k, (k + distance) % shards) for k in range(shards)]
        )

    squares = sum_of_squares(gradient, shards)
    parts = everyone(squares, "shard")
    parts = added(parts, lax.axis_size(GROUP))
    parts = everyone(parts, GROUP)
    grand_total = jnp.sum(parts[:, 0, 0])
    widened = gradient.astype(jnp.float32)
    clip_factor = jnp.minimum(
        1.0, clip_rms * math.sqrt(every_entry) / jnp.sqrt(grand_total + 1e-06)
    )
    fresh_state = (momentum_decay * momentum.astype(jnp.float32) + clip_factor * widened).astype(
        jnp.bfloat16
    )
    picked = fresh_state.reshape(paired.shape).at[slots].get(mode="promise_in_bounds")
    states = lax.all_to_all(picked, "shard", split_axis=0, concat_axis=0, tiled=True)
    sums = orthogonal(states, tokens[0, 0])

    prompt = jnp.moveaxis(tokens[0, 0].reshape(-1, shards, rows), 1, 0)
    early = tuple(d for d in old if d not in LATE)
    smem = pl.BlockSpec(memory_space=pltpu.SMEM)
    vmem = pl.BlockSpec(memory_space=pltpu.VMEM)
    count = prompt.shape[1]
    sums = pl.pallas_call(
        functools.partial(early_kernel, early),
        in_specs=[smem] + [vmem] * (2 + len(early)),
        out_specs=vmem,
        out_shape=jax.ShapeDtypeStruct((2, count, F), jnp.float32),
    )(at, prompt, sums, *(old[d] for d in early))
    hidden = pl.pallas_call(
        functools.partial(late_kernel, LATE),
        in_specs=[smem] + [vmem] * (2 + len(LATE)),
        out_specs=vmem,
        out_shape=jax.ShapeDtypeStruct((count, F), jnp.bfloat16),
    )(at, prompt, sums, *(old[d] for d in LATE))
    return (fresh_state, hidden[None, None])


def solution(mesh):
    split = Mesh(
        mesh.devices.reshape(mesh.shape["shard"], 4, 4, 2),
        ("shard", "group_0", "group_1", "group_2"),
    )
    placed = (
        P(GROUP, "shard", None),
        P(GROUP, "shard", None),
        P(GROUP, "shard", None),
        P(GROUP, None),
        P("shard", GROUP, None, None),
    )
    return jax.shard_map(
        step_and_prefill,
        mesh=split,
        in_specs=placed,
        out_specs=(P(GROUP, "shard", None), P("shard", GROUP, None, None)),
        check_vma=False,
    )
```
